256 devices in a mesh: dp: 4 (over z_lo), fsdp: 16 (over z_hi, x, core), tensor: 4 (over y).
Axes of the slice: x: 4, y: 4, z: 8 (z_hi: 2, z_lo: 4; z = z_hi * 4 + z_lo), core: 2. Of those that a mesh axis runs over, the one named last changes fastest.
Arguments:
- activations: bfloat16 [8192, 16384], P('dp', 'fsdp'), may hold values from -6 to 6
- out_grads: bfloat16 [8192, 26624], P('dp', 'tensor'), may hold values from -6 to 6
- weights: bfloat16 [16384, 26624], P(('fsdp', 'dp'), 'tensor'), may hold values from -6 to 6
- first_moment: float32 [256, 26624], P(('dp', 'fsdp'), 'tensor'), may hold values from -24 to 24
- second_moment: float32 [256, 26624], P(('dp', 'fsdp'), 'tensor'), may hold values from 32 to 512
- hash_seed: int32 [1], replicated, may hold values from 0 to 999999
- step_count: int32 [1], replicated, may hold values from 2 to 12
Outputs:
- update: bfloat16 [16384, 26624], P(('fsdp', 'dp'), 'tensor')
- first_new: float32 [256, 26624], P(('dp', 'fsdp'), 'tensor')
- second_new: float32 [256, 26624], P(('dp', 'fsdp'), 'tensor')
The draws below stay inside these ranges and needn't reach their ends.
All inputs are finite; a program needn't handle non-finite values.
Results may differ from the reference program's by a relative error of at most 0.029.
Values may be sent and summed in bfloat16 or wider, within the bound.
No kernel may reach another device: no remote copies, remote signals or barrier semaphores. Data moves between devices by JAX's collectives and lax.ppermute only.
A program may use at most 128 MiB of HBM per device.

```python
import math
import jax
import jax.numpy as jnp
from jax import lax

D = 16384
FF = 26624
RANK = 256
TOKENS = 8192


def steps_of(rng, shape, split, smallest, high):
    factor_of, own = 1.0, jax.random.fold_in(rng, 6)
    for position, blocks in split:
        draws = jnp.exp(jax.random.uniform(jax.random.fold_in(own, position), (blocks,), jnp.float32, smallest / len(split), high / len(split)))
        factor_of = factor_of * jnp.repeat(draws, shape[position] // blocks).reshape([-1 if axis == position else 1 for axis in range(len(shape))])
    return factor_of


def scatter_about(rng, dims, width, limit, cuts=(), kind=jnp.bfloat16):
    entries = jax.random.normal(rng, dims, jnp.float32) * width
    if len(cuts) > 0:
        entries = steps_of(rng, dims, cuts, -0.22, 0.18) * entries
    return jnp.clip(entries, min=-limit, max=limit).astype(kind)


def setup_inputs(seed: int = 0) -> dict:
    streams_of = jax.random.split(jax.random.key(seed), 8)
    activations = scatter_about(streams_of[0], (TOKENS, D), 1.0, 6.0, ((0, 4), (1, 16)))
    out_grads = scatter_about(streams_of[1], (TOKENS, FF), 1.0, 6.0, ((0, 4), (1, 4)))
    weights = scatter_about(streams_of[2], (D, FF), 1.0, 6.0, ((0, 64), (1, 4)))
    first_moment = scatter_about(streams_of[3], (RANK, FF), 4.0, 24.0, ((0, 64), (1, 4)), jnp.float32)
    second_moment = jnp.clip(jnp.exp(math.log(512.0) - 2.7725887 * jax.random.uniform(streams_of[4], (RANK, FF), jnp.float32) ** steps_of(streams_of[4], (RANK, FF), ((0, 64), (1, 4)), -0.2, 0.2)), 32.0, 512.0)
    hash_seed = jax.random.randint(streams_of[5], (1,), 0, 1000000).astype(jnp.int32)
    step_count = jax.random.randint(streams_of[6], (1,), 2, 13).astype(jnp.int32)
    return dict(activations=activations, out_grads=out_grads, weights=weights, first_moment=first_moment, second_moment=second_moment, hash_seed=hash_seed, step_count=step_count)


beta_first = 0.9
beta_second = 0.95
epsilon = 1e-08
decay_rate = 0.1

def omega_block(seed_scalar, row_first, row_total):
    row_ids = row_first + jnp.arange(row_total, dtype=jnp.int32)[:, None]
    col_ids = jnp.arange(RANK, dtype=jnp.int32)[None, :]
    hashed = row_ids * 73856093 ^ col_ids * 19349663 ^ seed_scalar * 83492791
    hashed = hashed ^ jnp.right_shift(hashed, 15)
    hashed = hashed * 1274126177
    hashed = hashed ^ jnp.right_shift(hashed, 13)
    hashed = hashed * 668265263
    hashed = hashed ^ jnp.right_shift(hashed, 16)
    summed = (hashed & 127) + (jnp.right_shift(hashed, 8) & 127) + (jnp.right_shift(hashed, 16) & 127) + (jnp.right_shift(hashed, 24) & 127)
    return (summed - 254).astype(jnp.float32).astype(jnp.bfloat16)

def right_solve(factor, matrix):
    return lax.linalg.triangular_solve(factor, matrix, left_side=False, lower=True, transpose_a=True)

def reference(activations, out_grads, weights, first_moment, second_moment, hash_seed, step_count):
    omega = omega_block(hash_seed[0], 0, FF)
    projected = jnp.dot(out_grads.astype(jnp.float32), omega.astype(jnp.float32), preferred_element_type=jnp.float32).astype(jnp.bfloat16)
    sketch = lax.dot_general(activations.astype(jnp.float32), projected.astype(jnp.float32), (((0,), (0,)), ((), ())), preferred_element_type=jnp.float32)
    gram_matrix = lax.dot_general(sketch, sketch, (((0,), (0,)), ((), ())), precision=lax.Precision.HIGHEST)
    factor = jnp.linalg.cholesky(gram_matrix)
    row_basis = right_solve(factor, sketch)
    coordinates = jnp.dot(activations.astype(jnp.float32), row_basis, precision=lax.Precision.HIGHEST).astype(jnp.bfloat16)
    coefficients = lax.dot_general(coordinates.astype(jnp.float32), out_grads.astype(jnp.float32), (((0,), (0,)), ((), ())), preferred_element_type=jnp.float32)
    first_new = beta_first * first_moment + (1.0 - beta_first) * coefficients
    second_new = beta_second * second_moment + (1.0 - beta_second) * coefficients * coefficients
    count_value = step_count[0].astype(jnp.float32)
    first_corr = 1.0 - jnp.power(jnp.float32(beta_first), count_value)
    second_corr = 1.0 - jnp.power(jnp.float32(beta_second), count_value)
    direction = (first_new / first_corr / (jnp.sqrt(second_new / second_corr) + epsilon)).astype(jnp.bfloat16)
    basis_half = row_basis.astype(jnp.bfloat16)
    update_scale = math.sqrt(D / RANK)
    product = jnp.dot(basis_half.astype(jnp.float32), direction.astype(jnp.float32), preferred_element_type=jnp.float32)
    update = (update_scale * product + decay_rate * weights.astype(jnp.float32)).astype(jnp.bfloat16)
    return (update, first_new, second_new)
```

```python
import math

import jax
import jax.numpy as jnp
from jax import lax
from jax.sharding import PartitionSpec as P

D = 16384
RANK = 256
F32, BF16 = jnp.float32, jnp.bfloat16
HIGHEST = lax.Precision.HIGHEST

beta_first = 0.9
beta_second = 0.95
epsilon = 1e-08
decay_rate = 0.1

PLACES = [(z, x, c) for z in range(2) for x in range(4) for c in range(2)]


def place(z, x, c):
    return (z % 2 * 4 + x % 4) * 2 + c % 2


SWAP_CORE = [(place(z, x, c), place(z, x, c + 1)) for z, x, c in PLACES]
SWAP_Z = [(place(z, x, c), place(z + 1, x, c)) for z, x, c in PLACES]
SHIFT_X = {s: [(place(z, x, c), place(z, x + s, c)) for z, x, c in PLACES] for s in (1, 2, 3)}
SHIFT_4 = {s: [(i, (i + s) % 4) for i in range(4)] for s in (1, 2, 3)}


def omega_block(seed_scalar, row_first, row_total):
    row_ids = row_first + jnp.arange(row_total, dtype=jnp.int32)[:, None]
    col_ids = jnp.arange(RANK, dtype=jnp.int32)[None, :]
    hashed = row_ids * 73856093 ^ col_ids * 19349663 ^ seed_scalar * 83492791
    hashed = hashed ^ jnp.right_shift(hashed, 15)
    hashed = hashed * 1274126177
    hashed = hashed ^ jnp.right_shift(hashed, 13)
    hashed = hashed * 668265263
    hashed = hashed ^ jnp.right_shift(hashed, 16)
    summed = (
        (hashed & 127)
        + (jnp.right_shift(hashed, 8) & 127)
        + (jnp.right_shift(hashed, 16) & 127)
        + (jnp.right_shift(hashed, 24) & 127)
    )
    return (summed - 254).astype(jnp.float32).astype(jnp.bfloat16)


def part(x, index, count, dim):
    size = x.shape[dim] // count
    return lax.dynamic_slice_in_dim(x, index * size, size, dim)


def scatter_4(x, axis, shifts, index, dim):
    got = {s: lax.ppermute(part(x, (index + s) % 4, 4, dim), axis, shifts[s]) for s in (1, 2, 3)}
    return (part(x, index, 4, dim) + got[2]) + (got[1] + got[3])


def exchange_4(x, axis, shifts):
    return [x] + [lax.ppermute(x, axis, shifts[s]) for s in (1, 2, 3)]


def gather_4(x, axis, shifts, index, dim):
    blocks = exchange_4(x, axis, shifts)
    size = x.shape[dim]
    shape = list(x.shape)
    shape[dim] = 4 * size
    out = jnp.zeros(shape, x.dtype)
    for s in range(4):
        out = lax.dynamic_update_slice_in_dim(out, blocks[s], (index - s) % 4 * size, dim)
    return out


def body(activations, out_grads, weights, first_moment, second_moment, hash_seed, step_count):
    f, y, dp = lax.axis_index("fsdp"), lax.axis_index("tensor"), lax.axis_index("dp")
    core, x, z = f % 2, f // 2 % 4, f // 8
    part_cols = out_grads.shape[1]

    omega = omega_block(hash_seed[0], y * part_cols, part_cols)
    projected = lax.dot_general(
        omega, out_grads, (((0,), (1,)), ((), ())), preferred_element_type=F32
    )
    projected = scatter_4(projected, "tensor", SHIFT_4, y, 1).astype(BF16)
    projected = gather_4(projected, "tensor", SHIFT_4, y, 1)

    sketch = lax.dot_general(
        projected, activations, (((1,), (0,)), ((), ())), preferred_element_type=F32
    )
    sketch_own = scatter_4(sketch, "dp", SHIFT_4, dp, 1)
    sketch = gather_4(sketch_own, "dp", SHIFT_4, dp, 1)

    gram = lax.dot_general(sketch, sketch, (((1,), (1,)), ((), ())), precision=HIGHEST)
    half = part(gram, core, 2, 0) + lax.ppermute(part(gram, 1 - core, 2, 0), "fsdp", SWAP_CORE)
    blocks = exchange_4(half, "fsdp", SHIFT_X)
    half = (blocks[0] + blocks[2]) + (blocks[1] + blocks[3])
    half = half + lax.ppermute(half, "fsdp", SWAP_Z)
    other = lax.ppermute(half, "fsdp", SWAP_CORE)
    low, high = jnp.where(core == 0, half, other), jnp.where(core == 0, other, half)
    gram = jnp.concatenate([low, high], axis=0)

    products = lax.dot_general(
        sketch, activations.astype(F32), (((1,), (1,)), ((), ())), precision=HIGHEST
    )
    products = part(products, core, 2, 1) + lax.ppermute(
        part(products, 1 - core, 2, 1), "fsdp", SWAP_CORE
    )
    products = scatter_4(products, "fsdp", SHIFT_X, x, 1)
    products = part(products, z, 2, 1) + lax.ppermute(
        part(products, 1 - z, 2, 1), "fsdp", SWAP_Z
    )

    factor = jnp.linalg.cholesky(gram)
    inverse = lax.linalg.triangular_solve(
        factor, jnp.eye(RANK, dtype=F32), left_side=True, lower=True
    )

    by_owner = inverse.reshape(4, 16, 4, RANK).transpose(1, 0, 2, 3).reshape(RANK, RANK)
    coordinates = jnp.dot(by_owner, products, precision=HIGHEST).astype(BF16)
    chosen = lax.all_to_all(coordinates.reshape(16, 16, 128), "fsdp", 0, 0, tiled=True)
    chosen = chosen.reshape(2, 4, 2, 16, 128).transpose(3, 2, 1, 0, 4).reshape(16, 2048)

    coefficients = jnp.dot(chosen, out_grads, preferred_element_type=F32).astype(BF16)
    got = {
        s: lax.ppermute(part(coefficients, (dp + s) % 4, 4, 0), "dp", SHIFT_4[s]) for s in (1, 2, 3)
    }
    coefficients = (part(coefficients, dp, 4, 0).astype(F32) + got[2].astype(F32)) + (
        got[1].astype(F32) + got[3].astype(F32)
    )

    first_new = beta_first * first_moment + (1.0 - beta_first) * coefficients
    second_new = beta_second * second_moment + (1.0 - beta_second) * coefficients * coefficients
    count_value = step_count[0].astype(F32)
    first_corr = 1.0 - jnp.power(jnp.float32(beta_first), count_value)
    second_corr = 1.0 - jnp.power(jnp.float32(beta_second), count_value)
    direction = (first_new / first_corr / (jnp.sqrt(second_new / second_corr) + epsilon)).astype(
        BF16
    )

    rows = jnp.concatenate(exchange_4(direction, "dp", SHIFT_4), axis=0)
    rows = jnp.concatenate([rows, lax.ppermute(rows, "fsdp", SWAP_Z)], axis=0)
    pieces = exchange_4(rows, "fsdp", SHIFT_X)
    others = [lax.ppermute(piece, "fsdp", SWAP_CORE) for piece in pieces]
    mine = jnp.concatenate(pieces, axis=0)
    others = jnp.concatenate(others, axis=0)

    j = jnp.arange(RANK, dtype=jnp.int32)
    row_of = (
        (dp - j // 4) % 4 * 64
        + place((z - j // 16) % 2, (x - j // 32) % 4, (core - j // 128) % 2) * 4
        + j % 4
    )
    order = (j[:, None] == row_of[None, :]).astype(BF16)
    basis_half = lax.dot_general(
        sketch_own, inverse, (((0,), (1,)), ((), ())), precision=HIGHEST
    ).astype(BF16)
    basis_half = jnp.dot(basis_half, order, preferred_element_type=F32).astype(BF16)
    product = jnp.dot(basis_half[:, :128], mine, preferred_element_type=F32) + jnp.dot(
        basis_half[:, 128:], others, preferred_element_type=F32
    )
    update_scale = math.sqrt(D / RANK)
    update = (update_scale * product + decay_rate * weights.astype(F32)).astype(BF16)
    return (update, first_new, second_new)


def solution(mesh):
    placed = (
        P("dp", "fsdp"),
        P("dp", "tensor"),
        P(("fsdp", "dp"), "tensor"),
        P(("dp", "fsdp"), "tensor"),
        P(("dp", "fsdp"), "tensor"),
        P(),
        P(),
    )
    return jax.shard_map(
        body,
        mesh=mesh,
        in_specs=placed,
        out_specs=(
            P(("fsdp", "dp"), "tensor"),
            P(("dp", "fsdp"), "tensor"),
            P(("dp", "fsdp"), "tensor"),
        ),
        check_vma=False,
    )
```

```python
import functools
import math

import jax
import jax.numpy as jnp
from jax import lax
from jax.experimental import pallas as pl
from jax.experimental.pallas import tpu as pltpu
from jax.sharding import PartitionSpec as P

D = 16384
RANK = 256
F32, BF16, I32 = jnp.float32, jnp.bfloat16, jnp.int32
HIGHEST = lax.Precision.HIGHEST
VMEM = pl.BlockSpec(memory_space=pltpu.VMEM)

beta_first = 0.9
beta_second = 0.95
epsilon = 1e-08
decay_rate = 0.1

PLACES = [(z, x, c) for z in range(2) for x in range(4) for c in range(2)]


def place(z, x, c):
    return (z % 2 * 4 + x % 4) * 2 + c % 2


SWAP_CORE = [(place(z, x, c), place(z, x, c + 1)) for z, x, c in PLACES]
SWAP_Z = [(place(z, x, c), place(z + 1, x, c)) for z, x, c in PLACES]
SHIFT_X = {s: [(place(z, x, c), place(z, x + s, c)) for z, x, c in PLACES] for s in (1, 2, 3)}
SHIFT_4 = {s: [(i, (i + s) % 4) for i in range(4)] for s in (1, 2, 3)}

SEED, UNIT, Y, CORE, DP, X, Z = range(7)


def struct(shape, dtype):
    return jax.ShapeDtypeStruct(shape, dtype)


def small_call(kernel, outs, name, flops=1 << 24, scratch=()):
    def call(info, *arrays):
        return pl.pallas_call(
            kernel,
            out_shape=outs,
            in_specs=[pl.BlockSpec(memory_space=pltpu.SMEM)] + [VMEM] * len(arrays),
            out_specs=jax.tree.map(lambda _: VMEM, outs),
            scratch_shapes=list(scratch),
            cost_estimate=pl.CostEstimate(flops=flops, bytes_accessed=1 << 20, transcendentals=0),
            name=name,
        )(info, *arrays)

    return call


DEPTH = 1664


def wrap(value):
    return (value + 2**31) % 2**32 - 2**31


def omega_tile(info_ref, step, base_ref, out_ref):
    first = (info_ref[UNIT] + step * DEPTH) * 73856093
    unit = lax.broadcasted_iota(I32, (8, RANK), 0) * 73856093
    mask = jnp.int32(0x007F007F)
    for k in range(0, DEPTH, 16):
        pair = []
        for q in (k, k + 8):
            h = (unit + (first + wrap(q * 73856093))) ^ base_ref[...]
            h = h ^ jnp.right_shift(h, 15)
            h = h * 1274126177
            h = h ^ jnp.right_shift(h, 13)
            h = h * 668265263
            h = h ^ jnp.right_shift(h, 16)
            two = (h & mask) + (jnp.right_shift(h, 8) & mask)
            four = (two & 0xFFFF) + jnp.right_shift(two, 16)
            pair.append((four - 254).astype(F32))
        out_ref[k : k + 16, :] = jnp.concatenate(pair, axis=0).astype(BF16)


def project_kernel(info_ref, grads_ref, out_ref, total, base, even, odd):
    step = pl.program_id(0)

    @pl.when(step == 0)
    def _():
        rank = lax.broadcasted_iota(I32, (8, RANK), 1)
        base[...] = rank * 19349663 ^ info_ref[SEED] * 83492791
        omega_tile(info_ref, 0, base, even)
        total[...] = jnp.zeros_like(total)

    def advance(now, later):
        omega_tile(info_ref, step + 1, base, later)
        total[...] += jnp.dot(grads_ref[...], now[...], preferred_element_type=F32)

    @pl.when(step % 2 == 0)
    def _():
        advance(even, odd)

    @pl.when(step % 2 == 1)
    def _():
        advance(odd, even)

    @pl.when(step == pl.num_programs(0) - 1)
    def _():
        out_ref[...] = total[...].T.astype(BF16)


def project(info, out_grads):
    tokens, units = out_grads.shape
    tokens = tokens // 2
    return pl.pallas_call(
        project_kernel,
        out_shape=struct((RANK, tokens), BF16),
        grid_spec=pltpu.PrefetchScalarGridSpec(
            num_scalar_prefetch=1,
            grid=(units // DEPTH,),
            in_specs=[pl.BlockSpec((tokens, DEPTH), lambda k, info: (info[CORE], k))],
            out_specs=pl.BlockSpec((RANK, tokens), lambda k, info: (0, 0)),
            scratch_shapes=[
                pltpu.VMEM((tokens, RANK), F32),
                pltpu.VMEM((8, RANK), I32),
                pltpu.VMEM((DEPTH, RANK), BF16),
                pltpu.VMEM((DEPTH, RANK), BF16),
            ],
        ),
        compiler_params=pltpu.CompilerParams(vmem_limit_bytes=32 << 20),
        cost_estimate=pl.CostEstimate(
            flops=2 * tokens * units * RANK, bytes_accessed=2 * tokens * units, transcendentals=0
        ),
        name="project",
    )(info, out_grads)


def sketch_kernel(info_ref, mine_ref, other_ref, acts_ref, *outs):
    core = info_ref[CORE]
    step = pl.program_id(0)
    half = mine_ref.shape[1]

    def rows(which):
        return acts_ref[pl.ds(pl.multiple_of(which * half, half), half), :]

    block = jnp.dot(mine_ref[...], rows(core), preferred_element_type=F32)
    block += jnp.dot(other_ref[...], rows(1 - core), preferred_element_type=F32)
    for shift in range(4):

        @pl.when(step == shift)
        def _():
            outs[shift][...] = block.astype(outs[shift].dtype)


def sketch_parts(info, mine, other, activations):
    tokens = activations.shape[0]
    whole = pl.BlockSpec((RANK, 256), lambda k, info: (0, 0))
    half = pl.BlockSpec((RANK, tokens // 2), lambda k, info: (0, 0))
    return pl.pallas_call(
        sketch_kernel,
        out_shape=(struct((RANK, 256), F32),) + (struct((RANK, 256), BF16),) * 3,
        grid_spec=pltpu.PrefetchScalarGridSpec(
            num_scalar_prefetch=1,
            grid=(4,),
            in_specs=[
                half,
                half,
                pl.BlockSpec((tokens, 256), lambda k, info: (0, (info[Y] + k) % 4)),
            ],
            out_specs=(whole,) * 4,
        ),
        cost_estimate=pl.CostEstimate(
            flops=2 * tokens * 1024 * RANK, bytes_accessed=2 * tokens * 1024, transcendentals=0
        ),
        name="sketch_parts",
    )(info, mine, other, activations)


def sum_cut_kernel(axis, info_ref, *refs):
    *blocks, total = refs
    ins, outs = blocks[:4], blocks[4:]
    total[...] = (ins[0][...].astype(F32) + ins[2][...].astype(F32)) + (
        ins[1][...].astype(F32) + ins[3][...].astype(F32)
    )
    cut(axis, info_ref, total, outs)


def cut(axis, info_ref, total, outs):
    size = outs[0].shape[0]
    for shift in range(4):
        who = (info_ref[axis] + shift) % 4
        outs[shift][...] = total[pl.ds(pl.multiple_of(who * size, size), size), :]


def add_cut_kernel(axis, info_ref, a_ref, b_ref, *refs):
    *outs, total = refs
    total[...] = a_ref[...] + b_ref[...]
    cut(axis, info_ref, total, outs)


def join_kernel(axis, info_ref, *refs):
    *ins, out_ref = refs
    size = ins[0].shape[0]
    for shift in range(4):
        who = (info_ref[axis] + 4 - shift) % 4
        out_ref[pl.ds(pl.multiple_of(who * size, size), size), :] = ins[shift][...]


def products_kernel(info_ref, *refs):
    pieces, (acts_ref, keep_ref, send_ref, own_ref, total) = refs[:4], refs[4:]
    y, core = info_ref[Y], info_ref[CORE]
    gram = products = None
    for shift in range(4):
        piece = pieces[shift][...]
        who = (y + 4 - shift) % 4
        columns = acts_ref[:, pl.ds(pl.multiple_of(who * 256, 256), 256)]
        more = lax.dot_general(piece, piece, (((1,), (1,)), ((), ())), preferred_element_type=F32)
        gram = more if gram is None else gram + more
        more = lax.dot_general(piece, columns, (((1,), (1,)), ((), ())), preferred_element_type=F32)
        products = more if products is None else products + more

        @pl.when(who == info_ref[DP])
        def _():
            own_ref[...] = piece

    total[:, :RANK] = gram
    total[:, RANK:] = products
    half = RANK // 2
    keep_ref[...] = total[pl.ds(pl.multiple_of(core * half, half), half), :]
    send_ref[...] = total[pl.ds(pl.multiple_of((1 - core) * half, half), half), :]


def gram_products(info, pieces, activations):
    tokens, depth = activations.shape
    tokens = tokens // 4
    square = pl.BlockSpec((RANK, 256), lambda i, info: (0, 0))
    wide = (RANK // 2, RANK + tokens)
    tall = pl.BlockSpec(wide, lambda i, info: (0, 0))
    return pl.pallas_call(
        products_kernel,
        out_shape=(struct(wide, F32), struct(wide, F32), struct((RANK, 256), BF16)),
        grid_spec=pltpu.PrefetchScalarGridSpec(
            num_scalar_prefetch=1,
            grid=(1,),
            in_specs=[square] * 4 + [pl.BlockSpec((tokens, depth), lambda i, info: (info[Y], 0))],
            out_specs=(tall, tall, square),
            scratch_shapes=[pltpu.VMEM((RANK, RANK + tokens), F32)],
        ),
        cost_estimate=pl.CostEstimate(flops=1 << 29, bytes_accessed=1 << 21, transcendentals=0),
        name="gram_products",
    )(info, *pieces, activations)


BLOCK = 32


def inverse_kernel(info_ref, mine_ref, other_ref, out_ref, work):
    rows = lax.broadcasted_iota(I32, (RANK, RANK), 0)
    cols = lax.broadcasted_iota(I32, (RANK, RANK), 1)
    half, core = RANK // 2, info_ref[CORE]
    work[pl.ds(pl.multiple_of(core * half, half), half), :RANK] = mine_ref[...]
    work[pl.ds(pl.multiple_of((1 - core) * half, half), half), :RANK] = other_ref[...]
    work[:, RANK:] = (rows == cols).astype(F32)
    small_row = lax.broadcasted_iota(I32, (BLOCK, 128), 0)
    small_col = lax.broadcasted_iota(I32, (BLOCK, 128), 1)
    all_rows = lax.broadcasted_iota(I32, (RANK, BLOCK), 0)
    sub = lax.broadcasted_iota(I32, (8, 128), 0)
    tiles_of = BLOCK // 8

    @pl.loop(0, RANK // BLOCK)
    def _(step):
        first = pl.multiple_of(step * BLOCK, BLOCK)
        panel = work[pl.ds(first, BLOCK), :]
        shift = jnp.where(first == 0, 0, RANK - first)
        square = pltpu.roll(panel[:, :RANK], shift, 1)[:, :128]
        t = jnp.where(small_col < BLOCK, square, (small_col - BLOCK == small_row).astype(F32))
        tiles = [t[8 * k : 8 * k + 8] for k in range(tiles_of)]
        for k in range(tiles_of):
            spread = [
                [
                    jnp.broadcast_to(tiles[q][:, 8 * k + i : 8 * k + i + 1], (8, 128))
                    for q in range(k, tiles_of)
                ]
                for i in range(8)
            ]
            mults, scale = [], None
            for i in range(8):
                pivot = jnp.broadcast_to(spread[i][0][i : i + 1, :], (8, 128))
                scale = pivot if scale is None else jnp.where(sub == i, pivot, scale)
                inv = 1.0 / pivot
                mult = [c * inv for c in spread[i]]
                mult[0] = jnp.where(sub > i, mult[0], 0.0)
                mults.append(mult)
                for j in range(i + 1, 8):
                    top = jnp.broadcast_to(spread[j][0][i : i + 1, :], (8, 128))
                    spread[j] = [c - m * top for c, m in zip(spread[j], mult)]
            for i in range(8):
                row = jnp.broadcast_to(tiles[k][i : i + 1, :], (8, 128))
                for q in range(k, tiles_of):
                    tiles[q] = tiles[q] - mults[i][q - k] * row
            tiles[k] = tiles[k] * lax.rsqrt(scale)
        small = jnp.concatenate(tiles, axis=0)[:, BLOCK : 2 * BLOCK]
        done = jnp.dot(small, panel, precision=HIGHEST, preferred_element_type=F32)
        out_ref[pl.ds(first, BLOCK), :] = done[:, RANK:]
        left = pltpu.roll(work[:, :RANK], shift, 1)[:, :BLOCK]
        below = lax.dot_general(
            left, small, (((1,), (1,)), ((), ())), precision=HIGHEST, preferred_element_type=F32
        )
        below = jnp.where(all_rows >= first + BLOCK, below, 0.0)
        work[...] -= jnp.dot(below, done, precision=HIGHEST, preferred_element_type=F32)


def choose_kernel(info_ref, inverse_ref, *refs):
    *pieces, out_ref = refs
    core, half = info_ref[CORE], RANK // 2
    owner = info_ref[Z] * 4 + info_ref[X]
    rows = []
    for shift in range(4):
        who = (info_ref[DP] + shift) % 4
        rows.append(inverse_ref[pl.ds(pl.multiple_of(who * 64 + owner * 8, 8), 8), :])
    rows = jnp.concatenate(rows, axis=0)
    low, high = rows[:, :half], rows[:, half:]
    mine = jnp.where(core == 0, low, high)
    other = jnp.where(core == 0, high, low)
    width = pieces[0].shape[1]
    for shift in range(4):
        block = jnp.dot(mine, pieces[shift][...], precision=HIGHEST, preferred_element_type=F32)
        block += jnp.dot(
            other, pieces[4 + shift][...], precision=HIGHEST, preferred_element_type=F32
        )
        out_ref[:, shift * width : (shift + 1) * width] = block.astype(BF16)


WIDE = 1664
TALL = 256


def coefficient_kernel(info_ref, chosen_ref, grads_ref, *refs):
    *outs, total = refs
    step = pl.program_id(0)
    more = jnp.dot(chosen_ref[...], grads_ref[...], preferred_element_type=F32)

    @pl.when(step == 0)
    def _():
        total[...] = more

    @pl.when(step > 0)
    def _():
        total[...] += more

    @pl.when(step == pl.num_programs(0) - 1)
    def _():
        for shift in range(4):
            outs[shift][...] = total[8 * shift : 8 * shift + 8, :].astype(outs[shift].dtype)


def coefficients_of(info, chosen, out_grads, part):
    tokens = out_grads.shape[0]
    small = pl.BlockSpec((8, WIDE), lambda k, info: (0, 0))
    each = tokens // 4 // TALL
    return pl.pallas_call(
        coefficient_kernel,
        out_shape=(struct((8, WIDE), F32),) + (struct((8, WIDE), BF16),) * 3,
        grid_spec=pltpu.PrefetchScalarGridSpec(
            num_scalar_prefetch=1,
            grid=(tokens // TALL,),
            in_specs=[
                pl.BlockSpec((32, TALL), lambda k, info: (0, k)),
                pl.BlockSpec(
                    (TALL, WIDE),
                    lambda k, info: (
                        (info[Y] + 4 - k // each) % 4 * each + k % each,
                        info[CORE] * 2 + part,
                    ),
                ),
            ],
            out_specs=(small,) * 4,
            scratch_shapes=[pltpu.VMEM((32, WIDE), F32)],
        ),
        cost_estimate=pl.CostEstimate(
            flops=2 * 256 * tokens * WIDE, bytes_accessed=2 * tokens * WIDE, transcendentals=0
        ),
        name="coefficients",
    )(info, chosen, out_grads)


def basis_kernel(info_ref, own_ref, inverse_ref, out_ref):
    basis = lax.dot_general(
        own_ref[...].astype(F32).T,
        inverse_ref[...],
        (((1,), (1,)), ((), ())),
        precision=HIGHEST,
        preferred_element_type=F32,
    ).astype(BF16)
    k = lax.broadcasted_iota(I32, (RANK, RANK), 1)
    rank = lax.broadcasted_iota(I32, (RANK, RANK), 0)
    x = (info_ref[X] + 4 - (k >> 6)) & 3
    z = (info_ref[Z] + 2 - ((k >> 5) & 1)) & 1
    dp = (info_ref[DP] + 4 - ((k >> 3) & 3)) & 3
    order = (rank == dp * 64 + (z * 4 + x) * 8 + (k & 7)).astype(F32).astype(BF16)
    out_ref[...] = jnp.dot(basis, order, preferred_element_type=F32).astype(BF16)


def update_kernel(info_ref, basis_ref, a_ref, b_ref, c_ref, d_ref, weights_ref, *refs):
    out_ref = refs[-1]
    direction = jnp.concatenate([a_ref[...], b_ref[...], c_ref[...], d_ref[...]], axis=0)
    product = jnp.dot(basis_ref[...], direction, preferred_element_type=F32)
    scale = math.sqrt(D / RANK)
    out_ref[...] = (scale * product + decay_rate * weights_ref[...].astype(F32)).astype(BF16)


def update_part(info, basis, pieces, weights, part, mine, before):
    rows, columns = weights.shape
    fixed = lambda shape: pl.BlockSpec(shape, lambda i, info: (0, 0))
    half = (lambda info: info[CORE]) if mine else (lambda info: 1 - info[CORE])
    block = pl.BlockSpec((rows, WIDE), lambda i, info: (0, half(info) * 2 + part))
    more = [] if before is None else [before]
    return pl.pallas_call(
        update_kernel,
        out_shape=struct((rows, columns), BF16),
        grid_spec=pltpu.PrefetchScalarGridSpec(
            num_scalar_prefetch=1,
            grid=(1,),
            in_specs=[fixed((RANK, RANK))]
            + [fixed((64, WIDE))] * 4
            + [block]
            + [pl.BlockSpec(memory_space=pl.ANY)] * len(more),
            out_specs=block,
        ),
        input_output_aliases={7: 0} if more else {},
        cost_estimate=pl.CostEstimate(
            flops=2 * rows * RANK * WIDE, bytes_accessed=4 * rows * WIDE, transcendentals=0
        ),
        name="update",
    )(info, basis, *pieces, weights, *more)


def shifts(blocks, axis, perms):
    return [blocks[0]] + [lax.ppermute(blocks[s], axis, perms[s]) for s in (1, 2, 3)]


def body(activations, out_grads, weights, first_moment, second_moment, hash_seed, step_count):
    f, y, dp = lax.axis_index("fsdp"), lax.axis_index("tensor"), lax.axis_index("dp")
    core, x, z = f % 2, f // 2 % 4, f // 8
    columns = out_grads.shape[1]
    info = jnp.stack([hash_seed[0], y * columns, y, core, dp, x, z]).astype(I32)
    swap = functools.partial(lax.ppermute, axis_name="fsdp", perm=SWAP_CORE)

    half = columns // 2
    moments = []
    for moment in (first_moment, second_moment):
        own = lax.dynamic_slice_in_dim(moment, core * half, half, 1)
        got = swap(lax.dynamic_slice_in_dim(moment, (1 - core) * half, half, 1))
        moments.append(
            jnp.concatenate([jnp.where(core == 0, own, got), jnp.where(core == 0, got, own)], 0)
        )

    projected = project(info, out_grads)
    parts = sketch_parts(info, projected, swap(projected), activations)

    parts = shifts(parts, "tensor", SHIFT_4)
    quarter = (struct((64, 256), F32),) * 4
    parts = small_call(
        functools.partial(sum_cut_kernel, DP), quarter, "sum_cut_dp", scratch=[pltpu.VMEM((256, 256), F32)]
    )(info, *parts)
    parts = shifts(parts, "dp", SHIFT_4)
    own = ((parts[0] + parts[2]) + (parts[1] + parts[3])).astype(BF16)
    parts = shifts([own] * 4, "dp", SHIFT_4)
    sketch = small_call(functools.partial(join_kernel, DP), struct((RANK, 256), BF16), "join_dp")(
        info, *parts
    )
    pieces = shifts([sketch] * 4, "tensor", SHIFT_4)

    keep, send, sketch_own = gram_products(info, pieces, activations)
    wide = keep.shape[1]
    eighth = (struct((32, wide), F32),) * 4
    parts = small_call(
        functools.partial(add_cut_kernel, X), eighth, "add_cut_x", scratch=[pltpu.VMEM((128, wide), F32)]
    )(info, keep, swap(send))
    parts = shifts(parts, "fsdp", SHIFT_X)
    own = (parts[0] + parts[2]) + (parts[1] + parts[3])
    own = own + lax.ppermute(own, "fsdp", SWAP_Z)
    parts = shifts([own] * 4, "fsdp", SHIFT_X)
    joined = small_call(functools.partial(join_kernel, X), struct((128, wide), F32), "join_x")(
        info, *parts
    )
    gram, products = joined[:, :RANK], joined[:, RANK:]
    inverse = small_call(
        inverse_kernel,
        struct((RANK, RANK), F32),
        "factor_inverse",
        flops=1 << 33,
        scratch=[pltpu.VMEM((RANK, 2 * RANK), F32)],
    )(info, gram, swap(gram))
    pieces = shifts([products] * 4, "tensor", SHIFT_4)
    pieces = pieces + [swap(piece) for piece in pieces]

    chosen = small_call(choose_kernel, struct((32, out_grads.shape[0]), BF16), "choose")(
        info, inverse, *pieces
    )
    basis = small_call(basis_kernel, struct((RANK, RANK), BF16), "basis")(info, sketch_own, inverse)

    count_value = step_count[0].astype(F32)
    first_corr = 1.0 - jnp.power(jnp.float32(beta_first), count_value)
    second_corr = 1.0 - jnp.power(jnp.float32(beta_second), count_value)

    update, firsts, seconds = None, [], []
    for part in range(2):
        parts = coefficients_of(info, chosen, out_grads, part)
        parts = shifts(parts, "dp", SHIFT_4)
        coefficients = (parts[0] + parts[2].astype(F32)) + (
            parts[1].astype(F32) + parts[3].astype(F32)
        )
        first, second = (m[:, part * WIDE : (part + 1) * WIDE] for m in moments)
        first_new = beta_first * first + (1.0 - beta_first) * coefficients
        second_new = beta_second * second + (1.0 - beta_second) * coefficients * coefficients
        direction = (
            first_new / first_corr / (jnp.sqrt(second_new / second_corr) + epsilon)
        ).astype(BF16)
        firsts.append(first_new)
        seconds.append(second_new)

        rows = jnp.concatenate(shifts([direction] * 4, "dp", SHIFT_4), axis=0)
        rows = jnp.concatenate([rows, lax.ppermute(rows, "fsdp", SWAP_Z)], axis=0)
        pieces = shifts([rows] * 4, "fsdp", SHIFT_X)
        others = [swap(piece) for piece in pieces]
        update = update_part(info, basis, pieces, weights, part, True, update)
        update = update_part(info, basis, others, weights, part, False, update)

    new_moments = []
    for parts in (firsts, seconds):
        both = jnp.concatenate(parts, axis=1)
        mine = lax.dynamic_slice_in_dim(both, core * 4, 4, 0)
        got = swap(lax.dynamic_slice_in_dim(both, (1 - core) * 4, 4, 0))
        new_moments.append(
            jnp.concatenate([jnp.where(core == 0, mine, got), jnp.where(core == 0, got, mine)], 1)
        )
    return (update, *new_moments)


def solution(mesh):
    placed = (
        P("dp", "fsdp"),
        P("dp", "tensor"),
        P(("fsdp", "dp"), "tensor"),
        P(("dp", "fsdp"), "tensor"),
        P(("dp", "fsdp"), "tensor"),
        P(),
        P(),
    )
    return jax.shard_map(
        body,
        mesh=mesh,
        in_specs=placed,
        out_specs=(
            P(("fsdp", "dp"), "tensor"),
            P(("dp", "fsdp"), "tensor"),
            P(("dp", "fsdp"), "tensor"),
        ),
        check_vma=False,
    )
```

```python
import math

import jax
import jax.numpy as jnp
from jax import lax
from jax.experimental import pallas as pl
from jax.experimental.pallas import tpu as pltpu
from jax.sharding import Mesh, PartitionSpec as P

D = 16384
RANK = 256
F32, BF16, I32 = jnp.float32, jnp.bfloat16, jnp.int32
HIGHEST = lax.Precision.HIGHEST
VMEM = pl.BlockSpec(memory_space=pltpu.VMEM)

beta_first = 0.9
beta_second = 0.95
epsilon = 1e-08
decay_rate = 0.1

SWAP = [(0, 1), (1, 0)]
SHIFT_4 = {s: [(i, (i + s) % 4) for i in range(4)] for s in (1, 2, 3)}

SEED, UNIT, Y, CORE, DP, X, Z = range(7)


def struct(shape, dtype):
    return jax.ShapeDtypeStruct(shape, dtype)


DEPTH = 1664


def wrap(value):
    return (value + 2**31) % 2**32 - 2**31


def omega_tile(info_ref, step, base_ref, out_ref):
    first = (info_ref[UNIT] + step * DEPTH) * 73856093
    unit = lax.broadcasted_iota(I32, (8, RANK), 0) * 73856093
    mask = jnp.int32(0x007F007F)
    for k in range(0, DEPTH, 16):
        pair = []
        for q in (k, k + 8):
            h = (unit + (first + wrap(q * 73856093))) ^ base_ref[...]
            h = h ^ jnp.right_shift(h, 15)
            h = h * 1274126177
            h = h ^ jnp.right_shift(h, 13)
            h = h * 668265263
            h = h ^ jnp.right_shift(h, 16)
            two = (h & mask) + (jnp.right_shift(h, 8) & mask)
            four = (two & 0xFFFF) + jnp.right_shift(two, 16)
            pair.append((four - 254).astype(F32))
        out_ref[k : k + 16, :] = jnp.concatenate(pair, axis=0).astype(BF16)


def project_kernel(info_ref, grads_ref, out_ref, total, base, even, odd):
    step = pl.program_id(0)

    @pl.when(step == 0)
    def _():
        rank = lax.broadcasted_iota(I32, (8, RANK), 1)
        base[...] = rank * 19349663 ^ info_ref[SEED] * 83492791
        omega_tile(info_ref, 0, base, even)
        total[...] = jnp.zeros_like(total)

    def advance(now, later):
        omega_tile(info_ref, step + 1, base, later)
        total[...] += jnp.dot(grads_ref[...], now[...], preferred_element_type=F32)

    @pl.when(step % 2 == 0)
    def _():
        advance(even, odd)

    @pl.when(step % 2 == 1)
    def _():
        advance(odd, even)

    @pl.when(step == pl.num_programs(0) - 1)
    def _():
        out_ref[...] = total[...].T.astype(BF16)


def project(info, out_grads):
    tokens, units = out_grads.shape
    tokens = tokens // 2
    return pl.pallas_call(
        project_kernel,
        out_shape=struct((RANK, tokens), BF16),
        grid_spec=pltpu.PrefetchScalarGridSpec(
            num_scalar_prefetch=1,
            grid=(units // DEPTH,),
            in_specs=[pl.BlockSpec((tokens, DEPTH), lambda k, info: (info[CORE], k))],
            out_specs=pl.BlockSpec((RANK, tokens), lambda k, info: (0, 0)),
            scratch_shapes=[
                pltpu.VMEM((tokens, RANK), F32),
                pltpu.VMEM((8, RANK), I32),
                pltpu.VMEM((DEPTH, RANK), BF16),
                pltpu.VMEM((DEPTH, RANK), BF16),
            ],
        ),
        compiler_params=pltpu.CompilerParams(vmem_limit_bytes=32 << 20),
        cost_estimate=pl.CostEstimate(
            flops=2 * tokens * units * RANK, bytes_accessed=2 * tokens * units, transcendentals=0
        ),
        name="project",
    )(info, out_grads)


def sketch_kernel(info_ref, mine_ref, other_ref, acts_ref, *outs):
    core = info_ref[CORE]
    step = pl.program_id(0)
    half = mine_ref.shape[1]

    def rows(which):
        return acts_ref[pl.ds(pl.multiple_of(which * half, half), half), :]

    block = jnp.dot(mine_ref[...], rows(core), preferred_element_type=F32)
    block += jnp.dot(other_ref[...], rows(1 - core), preferred_element_type=F32)
    for shift in range(4):

        @pl.when(step == shift)
        def _():
            outs[shift][...] = block.astype(outs[shift].dtype)


def sketch_parts(info, mine, other, activations):
    tokens = activations.shape[0]
    whole = pl.BlockSpec((RANK, 256), lambda k, info: (0, 0))
    half = pl.BlockSpec((RANK, tokens // 2), lambda k, info: (0, 0))
    return pl.pallas_call(
        sketch_kernel,
        out_shape=(struct((RANK, 256), F32),) + (struct((RANK, 256), BF16),) * 3,
        grid_spec=pltpu.PrefetchScalarGridSpec(
            num_scalar_prefetch=1,
            grid=(4,),
            in_specs=[
                half,
                half,
                pl.BlockSpec((tokens, 256), lambda k, info: (0, (info[Y] + k) % 4)),
            ],
            out_specs=(whole,) * 4,
        ),
        cost_estimate=pl.CostEstimate(
            flops=2 * tokens * 1024 * RANK, bytes_accessed=2 * tokens * 1024, transcendentals=0
        ),
        name="sketch_parts",
    )(info, mine, other, activations)


def products_kernel(info_ref, *refs):
    pieces, (acts_ref, keep_ref, send_ref, own_ref, total) = refs[:4], refs[4:]
    y, core = info_ref[Y], info_ref[CORE]
    gram = products = None
    for shift in range(4):
        piece = pieces[shift][...]
        who = (y + 4 - shift) % 4
        columns = acts_ref[:, pl.ds(pl.multiple_of(who * 256, 256), 256)]
        more = lax.dot_general(piece, piece, (((1,), (1,)), ((), ())), preferred_element_type=F32)
        gram = more if gram is None else gram + more
        more = lax.dot_general(piece, columns, (((1,), (1,)), ((), ())), preferred_element_type=F32)
        products = more if products is None else products + more

        @pl.when(who == info_ref[DP])
        def _():
            own_ref[...] = piece

    total[:, :RANK] = gram
    total[:, RANK:] = products
    half = RANK // 2
    keep_ref[...] = total[pl.ds(pl.multiple_of(core * half, half), half), :]
    send_ref[...] = total[pl.ds(pl.multiple_of((1 - core) * half, half), half), :]


def gram_products(info, pieces, activations):
    tokens, depth = activations.shape
    tokens = tokens // 4
    square = pl.BlockSpec((RANK, 256), lambda i, info: (0, 0))
    wide = (RANK // 2, RANK + tokens)
    tall = pl.BlockSpec(wide, lambda i, info: (0, 0))
    return pl.pallas_call(
        products_kernel,
        out_shape=(struct(wide, F32), struct(wide, F32), struct((RANK, 256), BF16)),
        grid_spec=pltpu.PrefetchScalarGridSpec(
            num_scalar_prefetch=1,
            grid=(1,),
            in_specs=[square] * 4 + [pl.BlockSpec((tokens, depth), lambda i, info: (info[Y], 0))],
            out_specs=(tall, tall, square),
            scratch_shapes=[pltpu.VMEM((RANK, RANK + tokens), F32)],
        ),
        cost_estimate=pl.CostEstimate(flops=1 << 29, bytes_accessed=1 << 21, transcendentals=0),
        name="gram_products",
    )(info, *pieces, activations)


BLOCK = 32


def split(value):
    high = value.astype(BF16)
    return high, (value - high.astype(F32)).astype(BF16)


def inverse_kernel(info_ref, mine_ref, other_ref, out_ref, chosen_ref, work):
    rows = lax.broadcasted_iota(I32, (RANK, RANK), 0)
    cols = lax.broadcasted_iota(I32, (RANK, RANK), 1)
    half, core = RANK // 2, info_ref[CORE]
    work[pl.ds(pl.multiple_of(core * half, half), half), :RANK] = mine_ref[:, :RANK]
    work[pl.ds(pl.multiple_of((1 - core) * half, half), half), :RANK] = other_ref[:, :RANK]
    work[:, RANK:] = (rows == cols).astype(F32)
    small_row = lax.broadcasted_iota(I32, (BLOCK, 128), 0)
    small_col = lax.broadcasted_iota(I32, (BLOCK, 128), 1)
    all_rows = lax.broadcasted_iota(I32, (RANK, BLOCK), 0)
    sub = lax.broadcasted_iota(I32, (8, 128), 0)
    tiles_of = BLOCK // 8

    @pl.loop(0, RANK // BLOCK)
    def _(step):
        first = pl.multiple_of(step * BLOCK, BLOCK)
        panel = work[pl.ds(first, BLOCK), :]
        shift = jnp.where(first == 0, 0, RANK - first)
        square = pltpu.roll(panel[:, :RANK], shift, 1)[:, :128]
        t = jnp.where(small_col < BLOCK, square, (small_col - BLOCK == small_row).astype(F32))
        tiles = [t[8 * k : 8 * k + 8] for k in range(tiles_of)]
        for k in range(tiles_of):
            spread = [
                [
                    jnp.broadcast_to(tiles[q][:, 8 * k + i : 8 * k + i + 1], (8, 128))
                    for q in range(k, tiles_of)
                ]
                for i in range(8)
            ]
            mults, scale = [], None
            for i in range(8):
                pivot = jnp.broadcast_to(spread[i][0][i : i + 1, :], (8, 128))
                scale = pivot if scale is None else jnp.where(sub == i, pivot, scale)
                inv = 1.0 / pivot
                mult = [c * inv for c in spread[i]]
                mult[0] = jnp.where(sub > i, mult[0], 0.0)
                mults.append(mult)
                for j in range(i + 1, 8):
                    top = jnp.broadcast_to(spread[j][0][i : i + 1, :], (8, 128))
                    spread[j] = [c - m * top for c, m in zip(spread[j], mult)]
            for i in range(8):
                row = jnp.broadcast_to(tiles[k][i : i + 1, :], (8, 128))
                for q in range(k, tiles_of):
                    tiles[q] = tiles[q] - mults[i][q - k] * row
            tiles[k] = tiles[k] * lax.rsqrt(scale)
        small = jnp.concatenate(tiles, axis=0)[:, BLOCK : 2 * BLOCK]
        done = jnp.dot(small, panel, precision=HIGHEST, preferred_element_type=F32)
        out_ref[pl.ds(first, BLOCK), :] = done[:, RANK:]
        left = pltpu.roll(work[:, :RANK], shift, 1)[:, :BLOCK]
        below = lax.dot_general(
            left, small, (((1,), (1,)), ((), ())), precision=HIGHEST, preferred_element_type=F32
        )
        below = jnp.where(all_rows >= first + BLOCK, below, 0.0)
        work[...] -= jnp.dot(below, done, precision=HIGHEST, preferred_element_type=F32)

    owner = info_ref[Z] * 4 + info_ref[X]
    rows = [
        out_ref[pl.ds(pl.multiple_of(dp * 64 + owner * 8, 8), 8), :] for dp in range(4)
    ]
    rows = jnp.concatenate(rows, axis=0)
    low, high = rows[:, :half], rows[:, half:]
    block = None
    for factor, ref in (
        (jnp.where(core == 0, low, high), mine_ref),
        (jnp.where(core == 0, high, low), other_ref),
    ):
        a, a_rest = split(factor)
        b, b_rest = split(ref[:, RANK:])
        for left, right in ((a, b), (a, b_rest), (a_rest, b)):
            more = jnp.dot(left, right, preferred_element_type=F32)
            block = more if block is None else block + more
    chosen_ref[...] = block.astype(BF16)


def factor_inverse(info, mine, other):
    rows, wide = mine.shape
    fixed = lambda shape: pl.BlockSpec(shape, lambda i, info: (0, 0))
    return pl.pallas_call(
        inverse_kernel,
        out_shape=(struct((RANK, RANK), F32), struct((32, wide - RANK), BF16)),
        grid_spec=pltpu.PrefetchScalarGridSpec(
            num_scalar_prefetch=1,
            grid=(1,),
            in_specs=[fixed((rows, wide))] * 2,
            out_specs=(fixed((RANK, RANK)), fixed((32, wide - RANK))),
            scratch_shapes=[pltpu.VMEM((RANK, 2 * RANK), F32)],
        ),
        cost_estimate=pl.CostEstimate(flops=1 << 34, bytes_accessed=1 << 20, transcendentals=0),
        name="factor_inverse",
    )(info, mine, other)


def coefficient_kernel(info_ref, chosen_ref, grads_ref, out_ref, total):
    step = pl.program_id(0)
    more = jnp.dot(chosen_ref[0], grads_ref[...], preferred_element_type=F32)

    @pl.when(step == 0)
    def _():
        total[...] = more

    @pl.when(step > 0)
    def _():
        total[...] += more

    @pl.when(step == pl.num_programs(0) - 1)
    def _():
        out_ref[...] = total[...].astype(BF16)


def coefficients_of(info, chosen, out_grads):
    tokens, columns = out_grads.shape
    tall, half = tokens // 4, columns // 2
    return pl.pallas_call(
        coefficient_kernel,
        out_shape=struct((32, half), BF16),
        grid_spec=pltpu.PrefetchScalarGridSpec(
            num_scalar_prefetch=1,
            grid=(4,),
            in_specs=[
                pl.BlockSpec((1, 32, tall), lambda k, info: (k, 0, 0)),
                pl.BlockSpec((tall, half), lambda k, info: (k, info[CORE])),
            ],
            out_specs=pl.BlockSpec((32, half), lambda k, info: (0, 0)),
            scratch_shapes=[pltpu.VMEM((32, half), F32)],
        ),
        compiler_params=pltpu.CompilerParams(vmem_limit_bytes=32 << 20),
        cost_estimate=pl.CostEstimate(
            flops=2 * 256 * tokens * half, bytes_accessed=2 * tokens * half, transcendentals=0
        ),
        name="coefficients",
    )(info, chosen, out_grads)


def basis_kernel(info_ref, own_ref, inverse_ref, out_ref):
    basis = lax.dot_general(
        own_ref[...].astype(F32).T,
        inverse_ref[...],
        (((1,), (1,)), ((), ())),
        precision=HIGHEST,
        preferred_element_type=F32,
    ).astype(BF16)
    k = lax.broadcasted_iota(I32, (RANK, RANK), 1)
    rank = lax.broadcasted_iota(I32, (RANK, RANK), 0)
    x = (info_ref[X] + 4 - (k >> 6)) & 3
    z, dp = (k >> 5) & 1, (k >> 3) & 3
    order = (rank == dp * 64 + (z * 4 + x) * 8 + (k & 7)).astype(F32).astype(BF16)
    out_ref[...] = jnp.dot(basis, order, preferred_element_type=F32).astype(BF16)


def update_kernel(info_ref, basis_ref, a_ref, b_ref, c_ref, d_ref, weights_ref, *refs):
    out_ref = refs[-1]
    direction = jnp.concatenate([a_ref[...], b_ref[...], c_ref[...], d_ref[...]], axis=0)
    product = jnp.dot(basis_ref[...], direction, preferred_element_type=F32)
    scale = math.sqrt(D / RANK)
    out_ref[...] = (scale * product + decay_rate * weights_ref[...].astype(F32)).astype(BF16)


def basis_of(info, own, inverse):
    fixed = pl.BlockSpec((RANK, RANK), lambda i, info: (0, 0))
    return pl.pallas_call(
        basis_kernel,
        out_shape=struct((RANK, RANK), BF16),
        grid_spec=pltpu.PrefetchScalarGridSpec(
            num_scalar_prefetch=1, grid=(1,), in_specs=[fixed] * 2, out_specs=fixed
        ),
        cost_estimate=pl.CostEstimate(flops=1 << 30, bytes_accessed=1 << 19, transcendentals=0),
        name="basis",
    )(info, own, inverse)


WIDE = 1664


def update_half(info, basis, pieces, weights, mine, before):
    rows, columns = weights.shape
    half = (lambda info: info[CORE]) if mine else (lambda info: 1 - info[CORE])
    block = pl.BlockSpec((rows, WIDE), lambda i, info: (0, half(info) * 2 + i))
    more = [] if before is None else [before]
    return pl.pallas_call(
        update_kernel,
        out_shape=struct((rows, columns), BF16),
        grid_spec=pltpu.PrefetchScalarGridSpec(
            num_scalar_prefetch=1,
            grid=(columns // 2 // WIDE,),
            in_specs=[pl.BlockSpec((RANK, RANK), lambda i, info: (0, 0))]
            + [pl.BlockSpec((64, WIDE), lambda i, info: (0, i))] * 4
            + [block]
            + [pl.BlockSpec(memory_space=pl.ANY)] * len(more),
            out_specs=block,
        ),
        input_output_aliases={7: 0} if more else {},
        cost_estimate=pl.CostEstimate(
            flops=rows * RANK * columns, bytes_accessed=2 * rows * columns, transcendentals=0
        ),
        name="update",
    )(info, basis, *pieces, weights, *more)


def shifts(blocks, axis):
    return [blocks[0]] + [lax.ppermute(blocks[s], axis, SHIFT_4[s]) for s in (1, 2, 3)]


def swap(block):
    return lax.ppermute(block, "core", SWAP)


def trade(blocks, axes):
    return lax.all_to_all(blocks, axes, 0, 0, tiled=True)


def collect(block, axes, count):
    return trade(jnp.broadcast_to(block[None], (count, *block.shape)), axes)


def halves(core, mine, other, dim):
    return jnp.concatenate(
        [jnp.where(core == 0, mine, other), jnp.where(core == 0, other, mine)], dim
    )


def body(activations, out_grads, weights, first_moment, second_moment, hash_seed, step_count):
    dp, z, x, core, y = (lax.axis_index(n) for n in ("dp", "z", "x", "core", "tensor"))
    columns = out_grads.shape[1]
    half = columns // 2
    info = jnp.stack([hash_seed[0], y * columns, y, core, dp, x, z]).astype(I32)

    both = jnp.concatenate([first_moment, second_moment], axis=0)
    own = lax.dynamic_slice_in_dim(both, core * half, half, 1)
    got = swap(lax.dynamic_slice_in_dim(both, (1 - core) * half, half, 1))
    first = halves(core, own[:4], got[:4], 0)
    second = halves(core, own[4:], got[4:], 0)

    projected = project(info, out_grads)
    parts = sketch_parts(info, projected, swap(projected), activations)

    parts = shifts(parts, "tensor")
    sketch = (parts[0] + parts[2].astype(F32)) + (parts[1].astype(F32) + parts[3].astype(F32))
    sketch = trade(sketch.reshape(4, 64, 256), "dp").sum(axis=0).astype(BF16)
    sketch = collect(sketch, "dp", 4).reshape(RANK, 256)
    pieces = shifts([sketch] * 4, "tensor")

    keep, send, sketch_own = gram_products(info, pieces, activations)
    rows, wide = keep.shape
    total = (keep + swap(send)).reshape(8, rows // 8, wide)
    total = trade(total, ("z", "x")).sum(axis=0)
    total = collect(total, ("z", "x"), 8).reshape(rows, wide)

    inverse, chosen = factor_inverse(info, total, swap(total))
    chosen = collect(chosen, "tensor", 4)
    basis = basis_of(info, sketch_own, inverse)

    coefficients = coefficients_of(info, chosen, out_grads)
    coefficients = trade(coefficients.reshape(4, 8, half), "dp").astype(F32).sum(axis=0)
    count_value = step_count[0].astype(F32)
    first_corr = 1.0 - jnp.power(jnp.float32(beta_first), count_value)
    second_corr = 1.0 - jnp.power(jnp.float32(beta_second), count_value)
    first_new = beta_first * first + (1.0 - beta_first) * coefficients
    second_new = beta_second * second + (1.0 - beta_second) * coefficients * coefficients
    direction = (first_new / first_corr / (jnp.sqrt(second_new / second_corr) + epsilon)).astype(
        BF16
    )

    rows = collect(direction, ("z", "dp"), 8).reshape(64, half)
    pieces = shifts([rows] * 4, "x")
    others = [swap(piece) for piece in pieces]
    update = update_half(info, basis, pieces, weights, True, None)
    update = update_half(info, basis, others, weights, False, update)

    both = jnp.concatenate([first_new, second_new], axis=0).reshape(2, 2, 4, half)
    own = lax.dynamic_index_in_dim(both, core, 1, keepdims=False)
    got = swap(lax.dynamic_index_in_dim(both, 1 - core, 1, keepdims=False))
    first_out, second_out = (halves(core, own[i], got[i], 1) for i in range(2))
    return (update, first_out, second_out)


def solution(mesh):
    mesh = Mesh(mesh.devices.reshape(4, 2, 4, 2, 4), ("dp", "z", "x", "core", "tensor"))
    fsdp = ("z", "x", "core")
    wide = P((*fsdp, "dp"), "tensor")
    moment = P(("dp", *fsdp), "tensor")
    return jax.shard_map(
        body,
        mesh=mesh,
        in_specs=(P("dp", fsdp), P("dp", "tensor"), wide, moment, moment, P(), P()),
        out_specs=(wide, moment, moment),
        check_vma=False,
    )
```

```python
import math

import jax
import jax.numpy as jnp
from jax import lax
from jax.experimental import pallas as pl
from jax.experimental.pallas import tpu as pltpu
from jax.sharding import Mesh, PartitionSpec as P

D = 16384
RANK = 256
F32, BF16, I32 = jnp.float32, jnp.bfloat16, jnp.int32
HIGHEST = lax.Precision.HIGHEST
VMEM = pl.BlockSpec(memory_space=pltpu.VMEM)

beta_first = 0.9
beta_second = 0.95
epsilon = 1e-08
decay_rate = 0.1

SWAP = [(0, 1), (1, 0)]
SHIFT_4 = {s: [(i, (i + s) % 4) for i in range(4)] for s in (1, 2, 3)}

SEED, UNIT, Y, CORE, DP, X, Z = range(7)


def struct(shape, dtype):
    return jax.ShapeDtypeStruct(shape, dtype)


DEPTH = 1664


def wrap(value):
    return (value + 2**31) % 2**32 - 2**31


def omega_tile(info_ref, step, base_ref, out_ref):
    first = (info_ref[UNIT] + step * DEPTH) * 73856093
    unit = lax.broadcasted_iota(I32, (8, RANK), 0) * 73856093
    mask = jnp.int32(0x007F007F)
    for k in range(0, DEPTH, 16):
        pair = []
        for q in (k, k + 8):
            h = (unit + (first + wrap(q * 73856093))) ^ base_ref[...]
            h = h ^ jnp.right_shift(h, 15)
            h = h * 1274126177
            h = h ^ jnp.right_shift(h, 13)
            h = h * 668265263
            h = h ^ jnp.right_shift(h, 16)
            two = (h & mask) + (jnp.right_shift(h, 8) & mask)
            four = (two & 0xFFFF) + jnp.right_shift(two, 16)
            pair.append((four - 254).astype(F32))
        out_ref[k : k + 16, :] = jnp.concatenate(pair, axis=0).astype(BF16)


def project_kernel(info_ref, grads_ref, out_ref, total, base, even, odd):
    step = pl.program_id(0)

    @pl.when(step == 0)
    def _():
        rank = lax.broadcasted_iota(I32, (8, RANK), 1)
        base[...] = rank * 19349663 ^ info_ref[SEED] * 83492791
        omega_tile(info_ref, 0, base, even)
        total[...] = jnp.zeros_like(total)

    def advance(now, later):
        omega_tile(info_ref, step + 1, base, later)
        total[...] += jnp.dot(grads_ref[...], now[...], preferred_element_type=F32)

    @pl.when(step % 2 == 0)
    def _():
        advance(even, odd)

    @pl.when(step % 2 == 1)
    def _():
        advance(odd, even)

    @pl.when(step == pl.num_programs(0) - 1)
    def _():
        out_ref[...] = total[...].T.astype(BF16)


def project(info, out_grads):
    tokens, units = out_grads.shape
    tokens = tokens // 2
    return pl.pallas_call(
        project_kernel,
        out_shape=struct((RANK, tokens), BF16),
        grid_spec=pltpu.PrefetchScalarGridSpec(
            num_scalar_prefetch=1,
            grid=(units // DEPTH,),
            in_specs=[pl.BlockSpec((tokens, DEPTH), lambda k, info: (info[CORE], k))],
            out_specs=pl.BlockSpec((RANK, tokens), lambda k, info: (0, 0)),
            scratch_shapes=[
                pltpu.VMEM((tokens, RANK), F32),
                pltpu.VMEM((8, RANK), I32),
                pltpu.VMEM((DEPTH, RANK), BF16),
                pltpu.VMEM((DEPTH, RANK), BF16),
            ],
        ),
        compiler_params=pltpu.CompilerParams(vmem_limit_bytes=32 << 20),
        cost_estimate=pl.CostEstimate(
            flops=2 * tokens * units * RANK, bytes_accessed=2 * tokens * units, transcendentals=0
        ),
        name="project",
    )(info, out_grads)


def sketch_kernel(info_ref, mine_ref, other_ref, acts_ref, *refs):
    *outs, total = refs
    core, half = info_ref[CORE], mine_ref.shape[1]

    def rows(which):
        return acts_ref[pl.ds(pl.multiple_of(which * half, half), half), :]

    total[...] = jnp.dot(mine_ref[...], rows(core), preferred_element_type=F32) + jnp.dot(
        other_ref[...], rows(1 - core), preferred_element_type=F32
    )
    for shift in range(4):
        who = (info_ref[Y] + shift) % 4
        block = total[:, pl.ds(pl.multiple_of(who * 256, 256), 256)]
        outs[shift][...] = block.astype(outs[shift].dtype)


def sketch_parts(info, mine, other, activations):
    tokens, depth = activations.shape
    return pl.pallas_call(
        sketch_kernel,
        out_shape=(struct((RANK, 256), F32),) + (struct((RANK, 256), BF16),) * 3,
        in_specs=[pl.BlockSpec(memory_space=pltpu.SMEM), VMEM, VMEM, VMEM],
        out_specs=(VMEM,) * 4,
        scratch_shapes=[pltpu.VMEM((RANK, depth), F32)],
        cost_estimate=pl.CostEstimate(
            flops=2 * tokens * depth * RANK, bytes_accessed=2 * tokens * depth, transcendentals=0
        ),
        name="sketch_parts",
    )(info, mine, other, activations)


def products_kernel(info_ref, *refs):
    pieces, (acts_ref, keep_ref, send_ref, own_ref, total) = refs[:4], refs[4:]
    y, core = info_ref[Y], info_ref[CORE]
    gram = products = None
    for shift in range(4):
        piece = pieces[shift][...]
        who = (y + 4 - shift) % 4
        columns = acts_ref[:, pl.ds(pl.multiple_of(who * 256, 256), 256)]
        more = lax.dot_general(piece, piece, (((1,), (1,)), ((), ())), preferred_element_type=F32)
        gram = more if gram is None else gram + more
        more = lax.dot_general(piece, columns, (((1,), (1,)), ((), ())), preferred_element_type=F32)
        products = more if products is None else products + more

        @pl.when(who == info_ref[DP])
        def _():
            own_ref[...] = piece

    total[:, :RANK] = gram
    total[:, RANK:] = products
    half = RANK // 2
    keep_ref[...] = total[pl.ds(pl.multiple_of(core * half, half), half), :]
    send_ref[...] = total[pl.ds(pl.multiple_of((1 - core) * half, half), half), :]


def gram_products(info, pieces, activations):
    tokens, depth = activations.shape
    tokens = tokens // 4
    square = pl.BlockSpec((RANK, 256), lambda i, info: (0, 0))
    wide = (RANK // 2, RANK + tokens)
    tall = pl.BlockSpec(wide, lambda i, info: (0, 0))
    return pl.pallas_call(
        products_kernel,
        out_shape=(struct(wide, F32), struct(wide, F32), struct((RANK, 256), BF16)),
        grid_spec=pltpu.PrefetchScalarGridSpec(
            num_scalar_prefetch=1,
            grid=(1,),
            in_specs=[square] * 4 + [pl.BlockSpec((tokens, depth), lambda i, info: (info[Y], 0))],
            out_specs=(tall, tall, square),
            scratch_shapes=[pltpu.VMEM((RANK, RANK + tokens), F32)],
        ),
        cost_estimate=pl.CostEstimate(flops=1 << 29, bytes_accessed=1 << 21, transcendentals=0),
        name="gram_products",
    )(info, *pieces, activations)


BLOCK = 32


def split(value):
    high = value.astype(BF16)
    return high, (value - high.astype(F32)).astype(BF16)


def inverse_kernel(info_ref, mine_ref, other_ref, out_ref, chosen_ref, work):
    rows = lax.broadcasted_iota(I32, (RANK, RANK), 0)
    cols = lax.broadcasted_iota(I32, (RANK, RANK), 1)
    half, core = RANK // 2, info_ref[CORE]
    work[pl.ds(pl.multiple_of(core * half, half), half), :RANK] = mine_ref[:, :RANK]
    work[pl.ds(pl.multiple_of((1 - core) * half, half), half), :RANK] = other_ref[:, :RANK]
    work[:, RANK:] = (rows == cols).astype(F32)
    small_row = lax.broadcasted_iota(I32, (BLOCK, 128), 0)
    small_col = lax.broadcasted_iota(I32, (BLOCK, 128), 1)
    all_rows = lax.broadcasted_iota(I32, (RANK, BLOCK), 0)
    sub = lax.broadcasted_iota(I32, (8, 128), 0)
    tiles_of = BLOCK // 8

    @pl.loop(0, RANK // BLOCK)
    def _(step):
        first = pl.multiple_of(step * BLOCK, BLOCK)
        panel = work[pl.ds(first, BLOCK), :]
        shift = jnp.where(first == 0, 0, RANK - first)
        square = pltpu.roll(panel[:, :RANK], shift, 1)[:, :128]
        t = jnp.where(small_col < BLOCK, square, (small_col - BLOCK == small_row).astype(F32))
        tiles = [t[8 * k : 8 * k + 8] for k in range(tiles_of)]
        for k in range(tiles_of):
            spread = [
                [
                    jnp.broadcast_to(tiles[q][:, 8 * k + i : 8 * k + i + 1], (8, 128))
                    for q in range(k, tiles_of)
                ]
                for i in range(8)
            ]
            mults, scale = [], None
            for i in range(8):
                pivot = jnp.broadcast_to(spread[i][0][i : i + 1, :], (8, 128))
                scale = pivot if scale is None else jnp.where(sub == i, pivot, scale)
                inv = 1.0 / pivot
                mult = [c * inv for c in spread[i]]
                mult[0] = jnp.where(sub > i, mult[0], 0.0)
                mults.append(mult)
                for j in range(i + 1, 8):
                    top = jnp.broadcast_to(spread[j][0][i : i + 1, :], (8, 128))
                    spread[j] = [c - m * top for c, m in zip(spread[j], mult)]
            for i in range(8):
                row = jnp.broadcast_to(tiles[k][i : i + 1, :], (8, 128))
                for q in range(k, tiles_of):
                    tiles[q] = tiles[q] - mults[i][q - k] * row
            tiles[k] = tiles[k] * lax.rsqrt(scale)
        small = jnp.concatenate(tiles, axis=0)[:, BLOCK : 2 * BLOCK]
        done = jnp.dot(small, panel, precision=HIGHEST, preferred_element_type=F32)
        out_ref[pl.ds(first, BLOCK), :] = done[:, RANK:]
        left = pltpu.roll(work[:, :RANK], shift, 1)[:, :BLOCK]
        below = lax.dot_general(
            left, small, (((1,), (1,)), ((), ())), precision=HIGHEST, preferred_element_type=F32
        )
        below = jnp.where(all_rows >= first + BLOCK, below, 0.0)
        work[...] -= jnp.dot(below, done, precision=HIGHEST, preferred_element_type=F32)

    owner = info_ref[Z] * 4 + info_ref[X]
    rows = [
        out_ref[pl.ds(pl.multiple_of(dp * 64 + owner * 8, 8), 8), :] for dp in range(4)
    ]
    rows = jnp.concatenate(rows, axis=0)
    low, high = rows[:, :half], rows[:, half:]
    block = None
    for factor, ref in (
        (jnp.where(core == 0, low, high), mine_ref),
        (jnp.where(core == 0, high, low), other_ref),
    ):
        a, a_rest = split(factor)
        b, b_rest = split(ref[:, RANK:])
        for left, right in ((a, b), (a, b_rest), (a_rest, b)):
            more = jnp.dot(left, right, preferred_element_type=F32)
            block = more if block is None else block + more
    for peer in range(4):
        chosen_ref[peer] = block.astype(BF16)


def factor_inverse(info, mine, other):
    rows, wide = mine.shape
    fixed = lambda shape: pl.BlockSpec(shape, lambda i, info: (0, 0))
    return pl.pallas_call(
        inverse_kernel,
        out_shape=(struct((RANK, RANK), F32), struct((4, 32, wide - RANK), BF16)),
        grid_spec=pltpu.PrefetchScalarGridSpec(
            num_scalar_prefetch=1,
            grid=(1,),
            in_specs=[fixed((rows, wide))] * 2,
            out_specs=(
                fixed((RANK, RANK)),
                pl.BlockSpec((4, 32, wide - RANK), lambda i, info: (0, 0, 0)),
            ),
            scratch_shapes=[pltpu.VMEM((RANK, 2 * RANK), F32)],
        ),
        cost_estimate=pl.CostEstimate(flops=1 << 34, bytes_accessed=1 << 20, transcendentals=0),
        name="factor_inverse",
    )(info, mine, other)


def coefficient_kernel(info_ref, chosen_ref, grads_ref, out_ref, total):
    step = pl.program_id(0)
    more = jnp.dot(chosen_ref[0], grads_ref[...], preferred_element_type=F32)

    @pl.when(step == 0)
    def _():
        total[...] = more

    @pl.when(step > 0)
    def _():
        total[...] += more

    @pl.when(step == pl.num_programs(0) - 1)
    def _():
        out_ref[...] = total[...].astype(BF16)


def coefficients_of(info, chosen, out_grads):
    tokens, columns = out_grads.shape
    tall, half = tokens // 4, columns // 2
    return pl.pallas_call(
        coefficient_kernel,
        out_shape=struct((32, half), BF16),
        grid_spec=pltpu.PrefetchScalarGridSpec(
            num_scalar_prefetch=1,
            grid=(4,),
            in_specs=[
                pl.BlockSpec((1, 32, tall), lambda k, info: (k, 0, 0)),
                pl.BlockSpec((tall, half), lambda k, info: (k, info[CORE])),
            ],
            out_specs=pl.BlockSpec((32, half), lambda k, info: (0, 0)),
            scratch_shapes=[pltpu.VMEM((32, half), F32)],
        ),
        compiler_params=pltpu.CompilerParams(vmem_limit_bytes=32 << 20),
        cost_estimate=pl.CostEstimate(
            flops=2 * 256 * tokens * half, bytes_accessed=2 * tokens * half, transcendentals=0
        ),
        name="coefficients",
    )(info, chosen, out_grads)


def basis_kernel(info_ref, own_ref, inverse_ref, out_ref):
    basis = lax.dot_general(
        own_ref[...].astype(F32).T,
        inverse_ref[...],
        (((1,), (1,)), ((), ())),
        precision=HIGHEST,
        preferred_element_type=F32,
    ).astype(BF16)
    k = lax.broadcasted_iota(I32, (RANK, RANK), 1)
    rank = lax.broadcasted_iota(I32, (RANK, RANK), 0)
    x = (info_ref[X] + 4 - (k >> 6)) & 3
    z, dp = (k >> 5) & 1, (k >> 3) & 3
    order = (rank == dp * 64 + (z * 4 + x) * 8 + (k & 7)).astype(F32).astype(BF16)
    out_ref[...] = jnp.dot(basis, order, preferred_element_type=F32).astype(BF16)


def update_kernel(info_ref, basis_ref, a_ref, b_ref, c_ref, d_ref, weights_ref, *refs):
    out_ref = refs[-1]
    direction = jnp.concatenate([a_ref[...], b_ref[...], c_ref[...], d_ref[...]], axis=0)
    product = jnp.dot(basis_ref[...], direction, preferred_element_type=F32)
    scale = math.sqrt(D / RANK)
    out_ref[...] = (scale * product + decay_rate * weights_ref[...].astype(F32)).astype(BF16)


def basis_of(info, own, inverse):
    fixed = pl.BlockSpec((RANK, RANK), lambda i, info: (0, 0))
    return pl.pallas_call(
        basis_kernel,
        out_shape=struct((RANK, RANK), BF16),
        grid_spec=pltpu.PrefetchScalarGridSpec(
            num_scalar_prefetch=1, grid=(1,), in_specs=[fixed] * 2, out_specs=fixed
        ),
        cost_estimate=pl.CostEstimate(flops=1 << 30, bytes_accessed=1 << 19, transcendentals=0),
        name="basis",
    )(info, own, inverse)


WIDE = 1664


def update_half(info, basis, pieces, weights, mine, before):
    rows, columns = weights.shape
    half = (lambda info: info[CORE]) if mine else (lambda info: 1 - info[CORE])
    block = pl.BlockSpec((rows, WIDE), lambda i, info: (0, half(info) * 2 + i))
    more = [] if before is None else [before]
    return pl.pallas_call(
        update_kernel,
        out_shape=struct((rows, columns), BF16),
        grid_spec=pltpu.PrefetchScalarGridSpec(
            num_scalar_prefetch=1,
            grid=(columns // 2 // WIDE,),
            in_specs=[pl.BlockSpec((RANK, RANK), lambda i, info: (0, 0))]
            + [pl.BlockSpec((64, WIDE), lambda i, info: (0, i))] * 4
            + [block]
            + [pl.BlockSpec(memory_space=pl.ANY)] * len(more),
            out_specs=block,
        ),
        input_output_aliases={7: 0} if more else {},
        cost_estimate=pl.CostEstimate(
            flops=rows * RANK * columns, bytes_accessed=2 * rows * columns, transcendentals=0
        ),
        name="update",
    )(info, basis, *pieces, weights, *more)


def shifts(blocks, axis):
    return [blocks[0]] + [lax.ppermute(blocks[s], axis, SHIFT_4[s]) for s in (1, 2, 3)]


def total_of(blocks):
    a, b, c, d = (block.astype(F32) for block in blocks)
    return (a + c) + (b + d)


def swap(block):
    return lax.ppermute(block, "core", SWAP)


def trade(blocks, axes):
    return lax.all_to_all(blocks, axes, 0, 0, tiled=True)


def collect(block, axes, count):
    return trade(jnp.broadcast_to(block[None], (count, *block.shape)), axes)


def halves(core, mine, other, dim):
    return jnp.concatenate(
        [jnp.where(core == 0, mine, other), jnp.where(core == 0, other, mine)], dim
    )


def body(activations, out_grads, weights, first_moment, second_moment, hash_seed, step_count):
    dp, z, x, core, y = (lax.axis_index(n) for n in ("dp", "z", "x", "core", "tensor"))
    columns = out_grads.shape[1]
    half = columns // 2
    info = jnp.stack([hash_seed[0], y * columns, y, core, dp, x, z]).astype(I32)

    both = jnp.concatenate([first_moment, second_moment], axis=0)
    own = lax.dynamic_slice_in_dim(both, core * half, half, 1)
    got = swap(lax.dynamic_slice_in_dim(both, (1 - core) * half, half, 1))
    first = halves(core, own[:4], got[:4], 0)
    second = halves(core, own[4:], got[4:], 0)

    projected = project(info, out_grads)
    parts = sketch_parts(info, projected, swap(projected), activations)

    parts = shifts(parts, "tensor")
    sketch = total_of(parts)
    sketch = total_of(shifts([sketch.astype(BF16)] * 4, "dp")).astype(BF16)
    pieces = shifts([sketch] * 4, "tensor")

    keep, send, sketch_own = gram_products(info, pieces, activations)
    total = keep + swap(send)
    gram, products = total[:, :RANK], total[:, RANK:].astype(BF16)
    gram = total_of(shifts([gram] * 4, "x"))
    products = total_of(shifts([products] * 4, "x")).astype(BF16)
    gram = gram + lax.ppermute(gram, "z", SWAP)
    products = products.astype(F32) + lax.ppermute(products, "z", SWAP).astype(F32)
    total = jnp.concatenate([gram, products], axis=1)

    inverse, chosen = factor_inverse(info, total, swap(total))
    chosen = trade(chosen, "tensor")
    basis = basis_of(info, sketch_own, inverse)

    coefficients = coefficients_of(info, chosen, out_grads)
    coefficients = trade(coefficients.reshape(4, 8, half), "dp").astype(F32).sum(axis=0)
    count_value = step_count[0].astype(F32)
    first_corr = 1.0 - jnp.power(jnp.float32(beta_first), count_value)
    second_corr = 1.0 - jnp.power(jnp.float32(beta_second), count_value)
    first_new = beta_first * first + (1.0 - beta_first) * coefficients
    second_new = beta_second * second + (1.0 - beta_second) * coefficients * coefficients
    direction = (first_new / first_corr / (jnp.sqrt(second_new / second_corr) + epsilon)).astype(
        BF16
    )

    rows = collect(direction, ("z", "dp"), 8).reshape(64, half)
    pieces = shifts([rows] * 4, "x")
    others = [swap(piece) for piece in pieces]
    update = update_half(info, basis, pieces, weights, True, None)
    update = update_half(info, basis, others, weights, False, update)

    both = jnp.concatenate([first_new, second_new], axis=0).reshape(2, 2, 4, half)
    own = lax.dynamic_index_in_dim(both, core, 1, keepdims=False)
    got = swap(lax.dynamic_index_in_dim(both, 1 - core, 1, keepdims=False))
    first_out, second_out = (halves(core, own[i], got[i], 1) for i in range(2))
    return (update, first_out, second_out)


def solution(mesh):
    mesh = Mesh(mesh.devices.reshape(4, 2, 4, 2, 4), ("dp", "z", "x", "core", "tensor"))
    fsdp = ("z", "x", "core")
    wide = P((*fsdp, "dp"), "tensor")
    moment = P(("dp", *fsdp), "tensor")
    return jax.shard_map(
        body,
        mesh=mesh,
        in_specs=(P("dp", fsdp), P("dp", "tensor"), wide, moment, moment, P(), P()),
        out_specs=(wide, moment, moment),
        check_vma=False,
    )
```
